1024 devices in a mesh: expert: 8 (over y, core), tensor: 32 (over z), dp: 4 (over x).
Axes of the slice: x: 4, y: 4, z: 32, core: 2. Of those that a mesh axis runs over, the one named last changes fastest.
Arguments:
- tokens: bfloat16 [1024, 4096], P(('expert', 'dp'), 'tensor'), may hold values from -6 to 6
- grad_out: bfloat16 [1024, 4096], P(('expert', 'dp'), 'tensor'), may hold values from -6 to 6
- route_weights: float32 [1024, 2], P(('expert', 'dp')), may hold values from 0.1 to 0.9
- expert_ids: int32 [1024, 2], P(('expert', 'dp')), may hold values from 0 to 7, all different within a row; in each aligned block of 32 rows (0 to 31, 32 to 63, ...) at most 16 rows name the same one
- w_gate: bfloat16 [8, 4096, 8192], P('expert', None, 'tensor'), may hold values from -0.1875 to 0.1875
- w_up: bfloat16 [8, 4096, 8192], P('expert', None, 'tensor'), may hold values from -0.09375 to 0.09375
- w_down: bfloat16 [8, 4096, 8192], P('expert', None, 'tensor'), may hold values from -0.09375 to 0.09375
Outputs:
- grad_tokens: float32 [1024, 4096], P(('expert', 'dp'), 'tensor')
- grad_gate: bfloat16 [8, 4096, 8192], P('expert', 'dp', 'tensor')
- grad_up: bfloat16 [8, 4096, 8192], P('expert', 'dp', 'tensor')
The draws below stay inside these ranges and needn't reach their ends.
Inputs may be any that keep to these rules, and one draw needn't show every extreme that they name: `expert_ids`: each row names 2 different experts. In each token block of 32 rows no expert is named by more than 16 rows, a bound that some block reaches.
All inputs are finite; a program needn't handle non-finite values.
Results may differ from the reference program's by a relative error of at most 0.009.
Values may be sent and summed in bfloat16 or wider, within the bound.
A program may use at most 32 MiB of HBM per device.

```python
import math
import jax
import jax.numpy as jnp
import numpy as np
from jax import lax

D = 4096
TOP = 2
FFW = 8192
TOK_DEV = 32
EXPERTS = 8
TOKENS = 1024
CAP = 16
ROW_GROUPS = 4
N_EXPERT = 8


def strengthened(array, own_key, source, target, shards_of, factor):
    def block_of(dim):
        return (jnp.arange(array.shape[dim]) // (array.shape[dim] // shards_of)).reshape((-1,) + (1,) * (array.ndim - 1 - dim))

    first = jax.random.permutation(own_key, shards_of)[block_of(target)]
    second = (block_of(target) + shards_of // 2) % shards_of
    return jnp.where((block_of(source) == first) | (block_of(source) == second), factor * array, array)


def block_levels(own_key, shape, cuts, least, top_value):
    level, own = 1.0, jax.random.fold_in(own_key, 6)
    for dim, shards_of in cuts:
        steps = jnp.exp(jax.random.uniform(jax.random.fold_in(own, dim), (shards_of,), jnp.float32, least / len(cuts), top_value / len(cuts)))
        level = level * jnp.repeat(steps, shape[dim] // shards_of).reshape([-1 if axis == dim else 1 for axis in range(len(shape))])
    return level


def shared_out(rng, own, number, rows, count, top, limit, slope):
    order = jax.random.permutation(rng, count)
    heavy_load, ordinary = load_shares(count, rows * top, limit, slope, True), load_shares(count, rows * top, limit, slope, False)
    places = jnp.arange(count)

    def named(tallies, turn):
        used = int((tallies > 0).sum())
        fixed = max(1, used // 4)
        passed = fixed + (places - fixed + turn * (used - fixed)) % max(1, count - fixed)
        return jnp.zeros((count,), jnp.int32).at[order[jnp.where(places < fixed, places, passed)]].set(jnp.asarray(tallies, jnp.int32))

    tallies = jnp.where(number % 4 == 0, named(heavy_load, number // 4), named(ordinary, number - number // 4 - 1))
    mixed = jax.random.permutation(jax.random.fold_in(own, 3), count)
    source_of, sink = mixed[0:count // 2 * 2:2], mixed[1:count // 2 * 2:2]
    room = jnp.minimum(tallies[source_of] - 1, limit - tallies[sink]) // 2
    room = jnp.where((source_of == order[0]) | (sink == order[0]) | (tallies[sink] == 0), 0, jnp.maximum(room, 0))
    passed = jax.random.randint(jax.random.fold_in(own, 4), (count // 2,), 0, 1 << 20) % (room + 1)
    tallies = tallies.at[source_of].add(-passed).at[sink].add(passed)
    labels = jnp.searchsorted(jnp.cumsum(tallies), jnp.arange(rows * top), side="right").astype(jnp.int32)
    table = labels.reshape(top, rows).T
    table = table[jax.random.permutation(jax.random.fold_in(own, 1), rows)]
    turn = jax.random.randint(jax.random.fold_in(own, 2), (rows, 1), 0, top)
    return jnp.take_along_axis(table, (jnp.arange(top)[None, :] + turn) % top, axis=1)


def load_shares(count, total, reach, lean, full):
    portions = [(1 << 20) // math.isqrt(rank ** lean) + 1 for rank in range(1, count + 1)]
    largest = reach if full else min(reach, max(-(-total // count), total * portions[0] // sum(portions)))
    least = 1 if total - largest >= count - 1 else 0
    counts, surplus = [largest] + [least] * (count - 1), total - largest - least * (count - 1)
    while surplus > 0:
        candidates = [i for i in range(1, count) if counts[i] < largest] or [i for i in range(1, count) if counts[i] < reach]
        pool, budget = sum([portions[i] for i in candidates]), surplus
        for i in candidates:
            more = min(reach - counts[i], max(1, budget * portions[i] // pool), surplus)
            counts[i] = counts[i] + more
            surplus = surplus - more
    return np.array(counts)


def scatter_about(own_key, extent, deviation, bound, pieces=(), kind=jnp.bfloat16):
    level = block_levels(own_key, extent, pieces, -0.22, 0.18) if pieces else 1.0
    drawn = jax.random.normal(own_key, extent, jnp.float32) * deviation * level
    return jnp.minimum(jnp.maximum(drawn, -bound), bound).astype(kind)


def gaussian_with(key, extent, spread, most, pieces, heavy, held_as=jnp.bfloat16):
    array = spread * jax.random.normal(key, extent, jnp.float32)
    if pieces:
        array = array * block_levels(key, extent, pieces, -0.22, 0.18)
    return jnp.clip(strengthened(array, jax.random.fold_in(key, 3), *heavy), -most, most).astype(held_as)


def setup_inputs(seed: int = 0) -> dict:
    keys = jax.random.split(jax.random.key(seed), 8)
    tokens = scatter_about(keys[0], (TOKENS, D), 1.0, 6.0, ((0, 32), (1, 32)))
    grad_out = scatter_about(keys[1], (TOKENS, D), 1.0, 6.0, ((0, 32), (1, 32)))
    route_weights = jnp.clip(0.1 + 0.79999997 * jax.random.uniform(keys[2], (TOKENS, TOP), jnp.float32) ** block_levels(keys[2], (TOKENS, TOP), ((0, 32),), -0.2, 0.2), 0.1, 0.9)
    expert_ids_keys = jax.random.split(jax.random.fold_in(keys[3], 1), TOKENS // TOK_DEV)
    expert_ids_turns = jax.random.permutation(jax.random.fold_in(keys[3], 3), TOKENS // TOK_DEV)
    expert_ids = jax.vmap(lambda own, number: shared_out(jax.random.fold_in(keys[3], 2), own, number, TOK_DEV, EXPERTS, TOP, CAP, 2))(expert_ids_keys, expert_ids_turns).reshape((TOKENS, TOP))
    w_gate = gaussian_with(keys[4], (EXPERTS, D, FFW), D ** -0.5, 0.1875, ((0, 8), (2, 32)), (2, 1, 32, 2.75))
    w_up = scatter_about(keys[5], (EXPERTS, D, FFW), D ** -0.5, 0.09375, ((0, 8), (2, 32)))
    w_down = scatter_about(keys[6], (EXPERTS, D, FFW), D ** -0.5, 0.09375, ((0, 8), (2, 32)))
    return {"tokens": tokens, "grad_out": grad_out, "route_weights": route_weights, "expert_ids": expert_ids, "w_gate": w_gate, "w_up": w_up, "w_down": w_down}


def slot_picker(expert_ids, n_experts, capacity, block_rows):
    num_blocks = expert_ids.shape[0] // block_rows
    flat_ids = expert_ids.reshape(num_blocks, -1)
    expert_range = jnp.arange(n_experts, dtype=jnp.int32)
    onehot = (flat_ids[:, :, None] == expert_range[None, None, :]).astype(jnp.int32)
    earlier = jnp.cumsum(onehot, axis=1) - onehot
    position = jnp.sum(earlier * onehot, axis=2)
    slot_range = jnp.arange(capacity, dtype=jnp.int32)
    chosen = (flat_ids[:, None, None, :] == expert_range[None, :, None, None]) & (position[:, None, None, :] == slot_range[None, None, :, None])
    return jnp.where(chosen, 1.0, 0.0).astype(jnp.float32)


def rounded(values):
    return lax.optimization_barrier(values.astype(jnp.bfloat16)).astype(jnp.float32)


def reference(tokens, grad_out, route_weights, expert_ids, w_gate, w_up, w_down):
    num_blocks = TOKENS // TOK_DEV
    per_block = TOK_DEV * TOP
    picker = jnp.transpose(slot_picker(expert_ids, EXPERTS, CAP, TOK_DEV), (1, 0, 2, 3))
    token_copies = jnp.repeat(tokens.astype(jnp.float32), TOP, axis=0).reshape(num_blocks, per_block, D)
    grad_copies = jnp.repeat(grad_out.astype(jnp.float32), TOP, axis=0)
    scaled = rounded(route_weights.reshape(-1, 1) * grad_copies).reshape(num_blocks, per_block, D)
    dims_inner = (((1,), (1,)), ((), ()))
    dims_outer = (((0,), (0,)), ((), ()))

    def one_expert(carry, inputs):
        pick_one, gate_w, up_w, down_w = inputs
        rows_x = jnp.einsum("bca,bad->bcd", pick_one, token_copies, precision=lax.Precision.HIGHEST).astype(jnp.bfloat16).reshape(-1, D)
        rows_dy = jnp.einsum("bca,bad->bcd", pick_one, scaled, precision=lax.Precision.HIGHEST).astype(jnp.bfloat16).reshape(-1, D)
        gate_pre = jnp.dot(rows_x, gate_w, preferred_element_type=jnp.float32)
        up_pre = jnp.dot(rows_x, up_w, preferred_element_type=jnp.float32)
        sigmoid_gate = jax.nn.sigmoid(gate_pre)
        activated = gate_pre * sigmoid_gate
        d_hidden = jnp.dot(rows_dy, down_w, preferred_element_type=jnp.float32)
        d_up = (d_hidden * activated).astype(jnp.bfloat16)
        d_gate = (d_hidden * up_pre * sigmoid_gate * (1.0 + gate_pre * (1.0 - sigmoid_gate))).astype(jnp.bfloat16)
        contribution = lax.dot_general(d_gate, gate_w, dims_inner, preferred_element_type=jnp.float32)
        contribution = contribution + lax.dot_general(d_up, up_w, dims_inner, preferred_element_type=jnp.float32)
        carry = carry + jnp.einsum("bca,bcd->bad", pick_one, contribution.reshape(num_blocks, CAP, D), precision=lax.Precision.HIGHEST)
        grouped_x = rows_x.reshape(N_EXPERT, ROW_GROUPS, CAP, D)
        grouped_gate = d_gate.reshape(N_EXPERT, ROW_GROUPS, CAP, FFW)
        grouped_up = d_up.reshape(N_EXPERT, ROW_GROUPS, CAP, FFW)
        total_gate = jnp.zeros((D, FFW), jnp.float32)
        total_up = jnp.zeros((D, FFW), jnp.float32)
        for group_idx in range(ROW_GROUPS):
            left_rows = grouped_x[:, group_idx].reshape(-1, D)
            gate_rows = grouped_gate[:, group_idx].reshape(-1, FFW)
            up_rows = grouped_up[:, group_idx].reshape(-1, FFW)
            total_gate = total_gate + rounded(lax.dot_general(left_rows, gate_rows, dims_outer, preferred_element_type=jnp.float32))
            total_up = total_up + rounded(lax.dot_general(left_rows, up_rows, dims_outer, preferred_element_type=jnp.float32))
        return carry, (total_gate.astype(jnp.bfloat16), total_up.astype(jnp.bfloat16))

    start_carry = jnp.zeros((num_blocks, per_block, D), jnp.float32)
    final_carry, stacked = lax.scan(one_expert, start_carry, (picker, w_gate, w_up, w_down))
    grad_tokens = final_carry.reshape(TOKENS, TOP, D).sum(axis=1)
    return grad_tokens, stacked[0], stacked[1]
```

```python
import functools

import jax
import jax.numpy as jnp
from jax import lax
from jax.experimental import pallas as pl
from jax.experimental.pallas import tpu as pltpu
from jax.sharding import PartitionSpec as P

STRIDE = 2
LINK = jnp.bfloat16
F32 = jnp.float32
BF16 = jnp.bfloat16
NT = (((1,), (1,)), ((), ()))
TN = (((0,), (0,)), ((), ()))


def remote(src, dst, send_sem, recv_sem, **where):
    return pltpu.make_async_remote_copy(
        src_ref=src,
        dst_ref=dst,
        send_sem=send_sem,
        recv_sem=recv_sem,
        device_id=where,
        device_id_type=pl.DeviceIdType.MESH,
    )


def kernel(
    sizes,
    tok_ref, dy_ref, ids_ref, rw_ref, wg_hbm, wu_hbm, wd_hbm,
    gt_ref, gg_hbm, gu_hbm,
    wg, wu, wd, agp, agm, dsp, rows, acc_g, acc_u, acc_d, dd, ddall, xall,
    cs, cr, sbuf, rr, own, gg, gu,
    w_sem, ag_ssem, ag_rsem, ds_sem, dr_sem, xs_sem, xr_sem, dds_sem, ddr_sem,
    cs_sem, cr_sem, rs_sem, rr_sem, out_sem,
):
    n_e, n_z, n_x, cap = sizes
    S = STRIDE
    H = n_z // 2
    K = H // S
    toks = tok_ref.shape[0]
    feat = tok_ref.shape[1]
    ff = wg.shape[1]
    n_rows = n_e * cap
    per_q = n_z // n_x
    me = lax.axis_index("expert")
    z = lax.axis_index("tensor")
    mq = lax.axis_index("dp")

    loads = [
        pltpu.make_async_copy(src.at[0], dst, w_sem.at[i])
        for i, (src, dst) in enumerate(((wg_hbm, wg), (wu_hbm, wu), (wd_hbm, wd)))
    ]
    for load in loads:
        load.start()

    barrier = pltpu.get_barrier_semaphore()
    partners = []
    for m in range(1, S + 1):
        partners.append({"tensor": lax.rem(z + m, n_z)})
        partners.append({"tensor": lax.rem(z + n_z - m, n_z)})
    for i in range(1, n_e):
        partners.append({"expert": lax.rem(me + i, n_e)})
    for i in range(1, n_x):
        partners.append({"dp": lax.rem(mq + i, n_x)})
    for where in partners:
        pl.semaphore_signal(barrier, inc=1, device_id=where, device_id_type=pl.DeviceIdType.MESH)

    agm[0, :, 0:feat] = tok_ref[...]
    agm[0, :, feat : 2 * feat] = dy_ref[...]

    row = lax.broadcasted_iota(jnp.int32, (n_rows, toks), 0)
    row_expert = row // cap
    row_slot = (row - row_expert * cap).astype(F32)
    first = ids_ref[0:1, :] == row_expert
    second = ids_ref[1:2, :] == row_expert
    named = jnp.where(first, 1.0, jnp.where(second, 1.0, 0.0)).astype(F32)
    before = lax.broadcasted_iota(jnp.int32, (toks, toks), 0)
    after = lax.broadcasted_iota(jnp.int32, (toks, toks), 1)
    earlier = jnp.where(before < after, 1.0, 0.0).astype(BF16)
    place = jnp.dot(named.astype(BF16), earlier, preferred_element_type=F32)
    pick_f = jnp.where(place == row_slot, named, 0.0)
    weight = jnp.where(first, rw_ref[0:1, :], rw_ref[1:2, :])
    p_col = jnp.sum(pick_f * weight, axis=1, keepdims=True)
    pick = pick_f.astype(BF16)
    eye = jnp.where(before == after, 1.0, 0.0).astype(BF16)
    pick_back = lax.dot_general(eye, pick, NT, preferred_element_type=F32).astype(BF16)

    pl.semaphore_wait(barrier, len(partners))

    def up(m):
        return lax.rem(z + m, n_z)

    def down(m):
        return lax.rem(z + n_z - m, n_z)

    sends = []

    def ag_copy(sign, j, m):
        dist = S * j + m
        if sign > 0:
            src = agm.at[0] if j == 0 else agp.at[S * j - 1]
            return remote(src, agp.at[dist - 1], ag_ssem.at[0, dist - 1], ag_rsem.at[0, dist - 1], tensor=up(m))
        return remote(agm.at[S * j], agm.at[dist], ag_ssem.at[1, dist], ag_rsem.at[1, dist], tensor=down(m))

    def ag_wait(sign, dist):
        if sign > 0:
            remote(agp.at[dist - 1], agp.at[dist - 1], ag_ssem.at[0, dist - 1], ag_rsem.at[0, dist - 1], tensor=up(1)).wait_recv()
        elif dist > 0:
            remote(agm.at[dist], agm.at[dist], ag_ssem.at[1, dist], ag_rsem.at[1, dist], tensor=up(1)).wait_recv()

    def batch_of(sign, j):
        return j if sign > 0 else K + j

    def dists_of(sign, j):
        return [S * j + s + (1 if sign > 0 else 0) for s in range(S)]

    me_rows = pl.ds(pl.multiple_of(me * cap, cap), cap)

    def exchange(src, dst, b, send_sem, recv_sem):
        for i in range(1, n_e):
            e = lax.rem(me + i, n_e)
            copy = remote(
                src.at[b, :, pl.ds(pl.multiple_of(e * cap, cap), cap), :],
                dst.at[b, :, me_rows, :],
                send_sem.at[b], recv_sem.at[b], expert=e,
            )
            copy.start()
        dst[b, :, me_rows, :] = src[b, :, me_rows, :]

    def exchange_desc(src, dst, b, send_sem, recv_sem):
        part = pl.ds(0, n_rows - cap)
        return remote(src.at[b, :, part, :], dst.at[b, :, part, :], send_sem.at[b], recv_sem.at[b],
                      expert=lax.rem(me + 1, n_e))

    def dispatch(sign, j):
        b = batch_of(sign, j)
        refs = []
        for dist in dists_of(sign, j):
            if not (sign > 0 and dist % S == 0) and not (sign < 0 and dist % S == 0):
                ag_wait(sign, dist)
            refs.append(agp[dist - 1] if sign > 0 else agm[dist])
        wide = jnp.concatenate(refs, axis=1)
        picked = jnp.dot(pick, wide, preferred_element_type=F32)
        for s in range(S):
            base = 2 * feat * s
            dsp[b, s, :, 0:feat] = picked[:, base : base + feat].astype(BF16)
            dsp[b, s, :, feat : 2 * feat] = (picked[:, base + feat : base + 2 * feat] * p_col).astype(BF16)
        exchange(dsp, rows, b, ds_sem, dr_sem)

    started = []

    def consume(sign, j):
        b = batch_of(sign, j)
        exchange_desc(dsp, rows, b, ds_sem, dr_sem).wait_recv()
        if not started:
            for load in loads:
                load.wait()
        places = [down(dist) if sign > 0 else up(dist) for dist in dists_of(sign, j)]
        x = jnp.concatenate([rows[b, s, :, 0:feat] for s in range(S)], axis=1)
        d = jnp.concatenate([rows[b, s, :, feat : 2 * feat] for s in range(S)], axis=1)

        def slab(w):
            return jnp.concatenate(
                [w[pl.ds(pl.multiple_of(at * feat, feat), feat), :] for at in places], axis=0)

        for lhs, w, acc in ((x, wg, acc_g), (x, wu, acc_u), (d, wd, acc_d)):
            term = jnp.dot(lhs, slab(w), preferred_element_type=F32)
            acc[...] = term if not started else acc[...] + term
        started.append(True)
        for s, at in enumerate(places):
            to = at // per_q
            local = lax.rem(at, per_q)

            @pl.when(to == mq)
            def _():
                xall[mq, local] = rows[b, s, :, 0:feat]

            if n_x > 1:
                @pl.when(to != mq)
                def _():
                    remote(rows.at[b, s, :, pl.ds(0, feat)], xall.at[mq, local], xs_sem.at[0],
                           xr_sem.at[mq], dp=to).start()

    for j in range(K):
        if j:
            ag_wait(1, S * j)
        for m in [S] + list(range(1, S)):
            copy = ag_copy(1, j, m)
            copy.start()
            sends.append(copy)
        if j:
            ag_wait(-1, S * j)
        for m in [S] + list(range(1, S)):
            if S * j + m < H:
                copy = ag_copy(-1, j, m)
                copy.start()
                sends.append(copy)
        if j >= 1:
            dispatch(1, j - 1)
            dispatch(-1, j - 1)
        if j >= 2:
            consume(1, j - 2)
            consume(-1, j - 2)
    dispatch(-1, K - 1)
    ag_wait(1, H)
    dispatch(1, K - 1)
    if K >= 2:
        consume(1, K - 2)
        consume(-1, K - 2)
    consume(-1, K - 1)
    consume(1, K - 1)

    gate_pre = acc_g[...]
    up_pre = acc_u[...]
    d_hidden = acc_d[...]
    sig = jax.nn.sigmoid(gate_pre)
    d_up = (d_hidden * (gate_pre * sig)).astype(BF16)
    d_gate = (d_hidden * up_pre * sig * (1.0 + gate_pre * (1.0 - sig))).astype(BF16)
    dd[:, 0:ff] = d_gate
    dd[:, ff : 2 * ff] = d_up
    ddall[mq] = dd[...]

    def contribute(sign, j):
        b = batch_of(sign, j)
        places = [up(dist) if sign > 0 else down(dist) for dist in dists_of(sign, j)]

        def slab(w):
            return jnp.concatenate(
                [w[pl.ds(pl.multiple_of(at * feat, feat), feat), :] for at in places], axis=0)

        part = lax.dot_general(dd[:, 0:ff], slab(wg), NT, preferred_element_type=F32)
        part = part + lax.dot_general(dd[:, ff : 2 * ff], slab(wu), NT, preferred_element_type=F32)
        for s in range(S):
            cs[b, s] = part[:, feat * s : feat * (s + 1)].astype(BF16)
        exchange(cs, cr, b, cs_sem, cr_sem)

    def ring_copy(sign, j, m):
        where = (up if sign > 0 else down)(S if m == 0 else m)
        d = 0 if sign > 0 else 1
        return remote(sbuf.at[d, j, m], rr.at[d, j, m], rs_sem.at[d, j, m], rr_sem.at[d, j, m], tensor=where)

    def combine(sign, j):
        b = batch_of(sign, j)
        d = 0 if sign > 0 else 1
        exchange_desc(cs, cr, b, cs_sem, cr_sem).wait_recv()
        wide = jnp.concatenate([cr[b, s] for s in range(S)], axis=1)
        comb = jnp.dot(pick_back, wide, preferred_element_type=F32)
        for s in range(S):
            piece = comb[:, feat * s : feat * (s + 1)]
            l = (s + 1) % S if sign > 0 else s
            if l == 0:
                own[d, j] = piece
            else:
                sbuf[d, j, l] = piece.astype(LINK)
                copy = ring_copy(sign, j, l)
                copy.start()
                sends.append(copy)

    def relay_sum(sign, j):
        d = 0 if sign > 0 else 1
        total = None
        if sign > 0 and j > 0:
            total = own[0, j - 1]
        elif sign < 0:
            total = own[1, j]
        if j < K:
            for l in range(1, S):
                ring_copy(sign, j, l).wait_recv()
                piece = rr[d, j, l].astype(F32)
                total = piece if total is None else total + piece
            if sign > 0 or j < K - 1:
                ring_copy(sign, j, 0).wait_recv()
                piece = rr[d, j, 0].astype(F32)
                total = piece if total is None else total + piece
        return total

    def relay(sign, j):
        d = 0 if sign > 0 else 1
        total = relay_sum(sign, j)
        sbuf[d, j - 1, 0] = total.astype(LINK)
        copy = ring_copy(sign, j - 1, 0)
        copy.start()
        sends.append(copy)

    def dd_desc(q):
        return remote(ddall.at[q], ddall.at[q], dds_sem.at[0], ddr_sem.at[q], dp=lax.rem(mq + 1, n_x))

    contribute(1, K - 1)
    contribute(-1, K - 1)
    for i in range(1, n_x):
        remote(ddall.at[mq], ddall.at[mq], dds_sem.at[0], ddr_sem.at[mq], dp=lax.rem(mq + i, n_x)).start()
    if K >= 2:
        contribute(1, K - 2)
        contribute(-1, K - 2)
    combine(1, K - 1)
    combine(-1, K - 1)

    state = {"slot": 0, "ready": False}

    def grads(count):
        if not state["ready"]:
            state["ready"] = True
            for i in range(1, n_x):
                q = lax.rem(mq + i, n_x)
                remote(xall.at[q], xall.at[q], xs_sem.at[0], xr_sem.at[q], dp=lax.rem(mq + 1, n_x)).wait_recv()
                dd_desc(q).wait_recv()
        for s in range(state["slot"], min(state["slot"] + count, per_q)):
            lhs = jnp.concatenate([xall[q, s] for q in range(n_x)], axis=0)
            rhs = jnp.concatenate([ddall[q] for q in range(n_x)], axis=0)
            out = lax.dot_general(lhs, rhs, TN, preferred_element_type=F32)
            gg[feat * s : feat * (s + 1), :] = out[:, 0:ff].astype(BF16)
            gu[feat * s : feat * (s + 1), :] = out[:, ff : 2 * ff].astype(BF16)
        state["slot"] = min(state["slot"] + count, per_q)

    late = max(1, K // 2)
    for j in range(K - 1, -1, -1):
        relay(1, j + 1)
        if j + 1 <= K - 1:
            relay(-1, j + 1)
        if j >= 1:
            combine(1, j - 1)
            combine(-1, j - 1)
        if j >= 2:
            contribute(1, j - 2)
            contribute(-1, j - 2)
        if j < late:
            grads(-(-per_q // late))
    outs = [
        pltpu.make_async_copy(gg, gg_hbm.at[0], out_sem.at[0]),
        pltpu.make_async_copy(gu, gu_hbm.at[0], out_sem.at[1]),
    ]
    for copy in outs:
        copy.start()
    gt_ref[...] = relay_sum(1, 0) + relay_sum(-1, 0)

    for copy in sends:
        copy.wait_send()
    for b in range(2 * K):
        exchange_desc(dsp, rows, b, ds_sem, dr_sem).wait_send()
        exchange_desc(cs, cr, b, cs_sem, cr_sem).wait_send()
    if n_x > 1:
        part = pl.ds(0, n_x - 1)
        remote(xall.at[part], xall.at[part], xs_sem.at[0], xr_sem.at[0], dp=lax.rem(mq + 1, n_x)).wait_send()
        remote(ddall.at[part], ddall.at[part], dds_sem.at[0], ddr_sem.at[0], dp=lax.rem(mq + 1, n_x)).wait_send()
    for copy in outs:
        copy.wait()


def body(tokens, grad_out, route_weights, expert_ids, w_gate, w_up, w_down):
    n_e, n_z, n_x = lax.axis_size("expert"), lax.axis_size("tensor"), lax.axis_size("dp")
    toks, feat = tokens.shape
    ff = w_gate.shape[2]
    width = w_gate.shape[1]
    cap = toks * expert_ids.shape[1] * 2 // n_e
    n_rows = n_e * cap
    S = STRIDE
    H = n_z // 2
    K = H // S
    per_q = n_z // n_x
    vmem = pl.BlockSpec(memory_space=pltpu.VMEM)
    hbm = pl.BlockSpec(memory_space=pl.ANY)
    dma = pltpu.SemaphoreType.DMA
    return pl.pallas_call(
        functools.partial(kernel, (n_e, n_z, n_x, cap)),
        name="moe_backward",
        out_shape=(
            jax.ShapeDtypeStruct((toks, feat), F32),
            jax.ShapeDtypeStruct((1, width // n_x, ff), BF16),
            jax.ShapeDtypeStruct((1, width // n_x, ff), BF16),
        ),
        in_specs=[vmem] * 4 + [hbm] * 3,
        out_specs=(vmem, hbm, hbm),
        scratch_shapes=[
            pltpu.VMEM((width, ff), BF16),
            pltpu.VMEM((width, ff), BF16),
            pltpu.VMEM((width, ff), BF16),
            pltpu.VMEM((H, toks, 2 * feat), BF16),
            pltpu.VMEM((H, toks, 2 * feat), BF16),
            pltpu.VMEM((2 * K, S, n_rows, 2 * feat), BF16),
            pltpu.VMEM((2 * K, S, n_rows, 2 * feat), BF16),
            pltpu.VMEM((n_rows, ff), F32),
            pltpu.VMEM((n_rows, ff), F32),
            pltpu.VMEM((n_rows, ff), F32),
            pltpu.VMEM((n_rows, 2 * ff), BF16),
            pltpu.VMEM((n_x, n_rows, 2 * ff), BF16),
            pltpu.VMEM((n_x, per_q, n_rows, feat), BF16),
            pltpu.VMEM((2 * K, S, n_rows, feat), BF16),
            pltpu.VMEM((2 * K, S, n_rows, feat), BF16),
            pltpu.VMEM((2, K, S, toks, feat), LINK),
            pltpu.VMEM((2, K, S, toks, feat), LINK),
            pltpu.VMEM((2, K, toks, feat), F32),
            pltpu.VMEM((width // n_x, ff), BF16),
            pltpu.VMEM((width // n_x, ff), BF16),
            dma((3,)),
            dma((2, H)), dma((2, H)),
            dma((2 * K,)), dma((2 * K,)),
            dma((1,)), dma((n_x,)),
            dma((1,)), dma((n_x,)),
            dma((2 * K,)), dma((2 * K,)),
            dma((2, K, S)), dma((2, K, S)),
            dma((2,)),
        ],
        compiler_params=pltpu.CompilerParams(collective_id=0, has_side_effects=True),
    )(tokens, grad_out, expert_ids.T, route_weights.T, w_gate, w_up, w_down)


def solution(mesh):
    placed = (
        P(("expert", "dp"), "tensor"),
        P(("expert", "dp"), "tensor"),
        P(("expert", "dp"), None),
        P(("expert", "dp"), None),
        P("expert", None, "tensor"),
        P("expert", None, "tensor"),
        P("expert", None, "tensor"),
    )
    return jax.shard_map(
        body,
        mesh=mesh,
        in_specs=placed,
        out_specs=(
            P(("expert", "dp"), "tensor"),
            P("expert", "dp", "tensor"),
            P("expert", "dp", "tensor"),
        ),
        check_vma=False,
    )
```

```python
import functools

import jax
import jax.numpy as jnp
from jax import lax
from jax.experimental import pallas as pl
from jax.experimental.pallas import tpu as pltpu
from jax.sharding import PartitionSpec as P

STRIDE = 4
LINK = jnp.bfloat16
F32 = jnp.float32
BF16 = jnp.bfloat16
NT = (((1,), (1,)), ((), ()))
TN = (((0,), (0,)), ((), ()))


def remote(src, dst, send_sem, recv_sem, **where):
    return pltpu.make_async_remote_copy(
        src_ref=src,
        dst_ref=dst,
        send_sem=send_sem,
        recv_sem=recv_sem,
        device_id=where,
        device_id_type=pl.DeviceIdType.MESH,
    )


def kernel(
    sizes,
    tok_hbm, dy_hbm, ids_hbm, rw_hbm, wg_hbm, wu_hbm, wd_hbm,
    gt_ref, gg, gu,
    tok_ref, dy_ref, ids_ref, rw_ref, wg, wu, wd, agp, agm, dsp, rows, acc_g, acc_u, acc_d, dd, ddall, xall,
    cs, cr, sbuf, rr, own,
    in_sem, w_sem, ag_ssem, ag_rsem, ds_sem, dr_sem, xs_sem, xr_sem, dds_sem, ddr_sem,
    cs_sem, cr_sem, rs_sem, rr_sem,
):
    n_e, n_z, n_x, cap = sizes
    S = STRIDE
    H = n_z // 2
    K = H // S
    toks = tok_hbm.shape[0]
    feat = tok_hbm.shape[1]
    ff = wg.shape[1]
    n_rows = n_e * cap
    per_q = n_z // n_x
    me = lax.axis_index("expert")
    z = lax.axis_index("tensor")
    mq = lax.axis_index("dp")

    firsts = [
        pltpu.make_async_copy(src, dst, in_sem.at[i])
        for i, (src, dst) in enumerate(((tok_hbm, tok_ref), (dy_hbm, dy_ref), (ids_hbm, ids_ref), (rw_hbm, rw_ref)))
    ]
    for load in firsts:
        load.start()
    loads = [
        pltpu.make_async_copy(src.at[0], dst, w_sem.at[i])
        for i, (src, dst) in enumerate(((wg_hbm, wg), (wu_hbm, wu), (wd_hbm, wd)))
    ]
    for load in loads:
        load.start()

    barrier = pltpu.get_barrier_semaphore()
    partners = []
    for m in range(1, S + 1):
        partners.append({"tensor": lax.rem(z + m, n_z)})
        partners.append({"tensor": lax.rem(z + n_z - m, n_z)})
    for i in range(1, n_e):
        partners.append({"expert": lax.rem(me + i, n_e)})
    for i in range(1, n_x):
        partners.append({"dp": lax.rem(mq + i, n_x)})
    for where in partners:
        pl.semaphore_signal(barrier, inc=1, device_id=where, device_id_type=pl.DeviceIdType.MESH)

    for load in firsts[:2]:
        load.wait()
    agm[0, :, 0:feat] = tok_ref[...]
    agm[0, :, feat : 2 * feat] = dy_ref[...]

    pl.semaphore_wait(barrier, len(partners))

    def up(m):
        return lax.rem(z + m, n_z)

    def down(m):
        return lax.rem(z + n_z - m, n_z)

    sends = []

    def ag_copy(sign, j, m):
        dist = S * j + m
        if sign > 0:
            src = agm.at[0] if j == 0 else agp.at[S * j - 1]
            return remote(src, agp.at[dist - 1], ag_ssem.at[0, dist - 1], ag_rsem.at[0, dist - 1], tensor=up(m))
        return remote(agm.at[S * j], agm.at[dist], ag_ssem.at[1, dist], ag_rsem.at[1, dist], tensor=down(m))

    def ag_wait(sign, dist):
        if sign > 0:
            remote(agp.at[dist - 1], agp.at[dist - 1], ag_ssem.at[0, dist - 1], ag_rsem.at[0, dist - 1], tensor=up(1)).wait_recv()
        elif dist > 0:
            remote(agm.at[dist], agm.at[dist], ag_ssem.at[1, dist], ag_rsem.at[1, dist], tensor=up(1)).wait_recv()

    def span(sign, part, j):
        if part:
            first, count = S * j + 1, S - 1
        else:
            first, count = (S * (j + 1) if sign > 0 else S * j), 1
        at = first - 1 if sign > 0 else H + first
        return first, count, at, (0 if sign > 0 else 2 * K) + 2 * j + part

    def dists_of(sign, part, j):
        first, count, _, _ = span(sign, part, j)
        return list(range(first, first + count))

    me_rows = pl.ds(pl.multiple_of(me * cap, cap), cap)

    def exchange(src, dst, group, send_sem, recv_sem):
        _, count, at, g = group
        held = pl.ds(at, count)
        for i in range(1, n_e):
            e = lax.rem(me + i, n_e)
            copy = remote(
                src.at[held, pl.ds(pl.multiple_of(e * cap, cap), cap), :],
                dst.at[held, me_rows, :],
                send_sem.at[g], recv_sem.at[g], expert=e,
            )
            copy.start()
        dst[at : at + count, me_rows, :] = src[at : at + count, me_rows, :]

    def exchange_desc(src, dst, group, send_sem, recv_sem):
        _, count, at, g = group
        held, part = pl.ds(at, count), pl.ds(0, n_rows - cap)
        return remote(src.at[held, part, :], dst.at[held, part, :], send_sem.at[g], recv_sem.at[g],
                      expert=lax.rem(me + 1, n_e))

    handed = {S * j + S - 1 for j in range(K - 1)} if S > 2 else set()

    def hand_copy(sign, dist):
        at = slot(sign, dist)[2]
        return remote(rows.at[slot(sign, dist - 1)[2]], rows.at[at], ds_sem.at[at], dr_sem.at[at],
                      tensor=(up if sign > 0 else down)(1))

    arrived = set()

    def await_rows(sign, dist):
        if (sign, dist) in arrived:
            return
        arrived.add((sign, dist))
        if dist in handed:
            hand_copy(sign, dist).wait_recv()
        else:
            exchange_desc(dsp, rows, slot(sign, dist), ds_sem, dr_sem).wait_recv()

    def hand(sign, dist):
        await_rows(sign, dist - 1)
        copy = hand_copy(sign, dist)
        copy.start()
        sends.append(copy)

    def slot(sign, dist):
        at = dist - 1 if sign > 0 else H + dist
        return dist, 1, at, at

    def dispatch(sign, dist):
        group = slot(sign, dist)
        at = group[2]
        picked = jnp.dot(pick, agp[dist - 1] if sign > 0 else agm[dist], preferred_element_type=F32)
        dsp[at, :, 0:feat] = picked[:, 0:feat].astype(BF16)
        dsp[at, :, feat : 2 * feat] = (picked[:, feat : 2 * feat] * p_col).astype(BF16)
        exchange(dsp, rows, group, ds_sem, dr_sem)

    started = []

    def consume(sign, j):
        parts = (1, 0) if sign > 0 else (0, 1)
        dists = [dist for part in parts for dist in dists_of(sign, part, j)]
        for dist in dists:
            await_rows(sign, dist)
        at0 = slot(sign, dists[0])[2]
        if not started:
            for load in loads:
                load.wait()
        places = [down(dist) if sign > 0 else up(dist) for dist in dists]
        x = jnp.concatenate([rows[at0 + s, :, 0:feat] for s in range(S)], axis=1)
        d = jnp.concatenate([rows[at0 + s, :, feat : 2 * feat] for s in range(S)], axis=1)

        def slab(w):
            return jnp.concatenate(
                [w[pl.ds(pl.multiple_of(at * feat, feat), feat), :] for at in places], axis=0)

        for lhs, w, acc in ((x, wg, acc_g), (x, wu, acc_u), (d, wd, acc_d)):
            term = jnp.dot(lhs, slab(w), preferred_element_type=F32)
            acc[...] = term if not started else acc[...] + term
        started.append(True)
        for s, at in enumerate(places):
            to = at // per_q
            local = lax.rem(at, per_q)

            @pl.when(to == mq)
            def _():
                xall[mq, local] = rows[at0 + s, :, 0:feat]

            if n_x > 1:
                @pl.when(to != mq)
                def _():
                    remote(rows.at[at0 + s, :, pl.ds(0, feat)], xall.at[mq, local], xs_sem.at[0],
                           xr_sem.at[mq], dp=to).start()

    def ag_send(sign, j, m):
        if sign > 0 or S * j + m < H:
            copy = ag_copy(sign, j, m)
            copy.start()
            sends.append(copy)

    def ag_step(j):
        for sign in (1, -1):
            if j:
                ag_wait(sign, S * j)
            ag_send(sign, j, S)
        for m in range(1, S):
            for sign in (1, -1):
                if S * j + m not in handed:
                    ag_send(sign, j, m)

    def spread(j):
        if j:
            dispatch(1, S * j)
        dispatch(-1, S * j)
        for m in range(1, S):
            for sign in (1, -1):
                if S * j + m not in handed:
                    ag_wait(sign, S * j + m)
                    dispatch(sign, S * j + m)
        if j and S * j - 1 in handed:
            for sign in (1, -1):
                hand(sign, S * j - 1)

    ag_step(0)
    for load in firsts[2:]:
        load.wait()
    row = lax.broadcasted_iota(jnp.int32, (n_rows, toks), 0)
    row_expert = row // cap
    row_slot = (row - row_expert * cap).astype(F32)
    first = ids_ref[0:1, :] == row_expert
    second = ids_ref[1:2, :] == row_expert
    named = jnp.where(first, 1.0, jnp.where(second, 1.0, 0.0)).astype(F32)
    before = lax.broadcasted_iota(jnp.int32, (toks, toks), 0)
    after = lax.broadcasted_iota(jnp.int32, (toks, toks), 1)
    earlier = jnp.where(before < after, 1.0, 0.0).astype(BF16)
    place = jnp.dot(named.astype(BF16), earlier, preferred_element_type=F32)
    pick_f = jnp.where(place == row_slot, named, 0.0)
    weight = jnp.where(first, rw_ref[0:1, :], rw_ref[1:2, :])
    p_col = jnp.sum(pick_f * weight, axis=1, keepdims=True)
    pick = pick_f.astype(BF16)
    eye = jnp.where(before == after, 1.0, 0.0).astype(BF16)
    pick_back = lax.dot_general(eye, pick, NT, preferred_element_type=F32).astype(BF16)

    spread(0)
    for j in range(1, K):
        ag_step(j)
        spread(j)
    for j in range(K // 2):
        consume(-1, j)
        consume(1, j)
    ag_wait(1, H)
    dispatch(1, H)
    for j in range(K // 2, K):
        consume(-1, j)
        consume(1, j)

    gate_pre = acc_g[...]
    up_pre = acc_u[...]
    d_hidden = acc_d[...]
    sig = jax.nn.sigmoid(gate_pre)
    d_up = (d_hidden * (gate_pre * sig)).astype(BF16)
    d_gate = (d_hidden * up_pre * sig * (1.0 + gate_pre * (1.0 - sig))).astype(BF16)
    dd[:, 0:ff] = d_gate
    dd[:, ff : 2 * ff] = d_up
    ddall[mq] = dd[...]

    def contribute(sign, part, j):
        group = span(sign, part, j)
        _, count, at, _ = group
        places = [up(dist) if sign > 0 else down(dist) for dist in dists_of(sign, part, j)]

        def slab(w):
            slabs = [w[pl.ds(pl.multiple_of(to * feat, feat), feat), :] for to in places]
            return jnp.concatenate(slabs, axis=0) if count > 1 else slabs[0]

        term = lax.dot_general(dd[:, 0:ff], slab(wg), NT, preferred_element_type=F32)
        term = term + lax.dot_general(dd[:, ff : 2 * ff], slab(wu), NT, preferred_element_type=F32)
        for s in range(count):
            cs[at + s] = term[:, feat * s : feat * (s + 1)].astype(BF16)
        exchange(cs, cr, group, cs_sem, cr_sem)

    def ring_copy(sign, j, m):
        where = (up if sign > 0 else down)(S if m == 0 else m)
        d = 0 if sign > 0 else 1
        return remote(sbuf.at[d, j, m], rr.at[d, j, m], rs_sem.at[d, j, m], rr_sem.at[d, j, m], tensor=where)

    def combine(sign, part, j):
        group = span(sign, part, j)
        _, count, at, _ = group
        d = 0 if sign > 0 else 1
        exchange_desc(cs, cr, group, cs_sem, cr_sem).wait_recv()
        wide = jnp.concatenate([cr[at + s] for s in range(count)], axis=1) if count > 1 else cr[at]
        comb = jnp.dot(pick_back, wide, preferred_element_type=F32)
        if not part:
            own[d, j] = comb
            return
        for s in range(count):
            sbuf[d, j, s + 1] = comb[:, feat * s : feat * (s + 1)].astype(LINK)
            copy = ring_copy(sign, j, s + 1)
            copy.start()
            sends.append(copy)

    def relay_sum(sign, j):
        d = 0 if sign > 0 else 1
        total = None
        if sign > 0 and j > 0:
            total = own[0, j - 1]
        elif sign < 0:
            total = own[1, j]
        if j < K:
            for l in range(1, S):
                ring_copy(sign, j, l).wait_recv()
                piece = rr[d, j, l].astype(F32)
                total = piece if total is None else total + piece
            if sign > 0 or j < K - 1:
                ring_copy(sign, j, 0).wait_recv()
                piece = rr[d, j, 0].astype(F32)
                total = piece if total is None else total + piece
        return total

    def relay(sign, j):
        d = 0 if sign > 0 else 1
        total = relay_sum(sign, j)
        sbuf[d, j - 1, 0] = total.astype(LINK)
        copy = ring_copy(sign, j - 1, 0)
        copy.start()
        sends.append(copy)

    def dd_desc(q):
        return remote(ddall.at[q], ddall.at[q], dds_sem.at[0], ddr_sem.at[q], dp=lax.rem(mq + 1, n_x))

    state = {"slot": 0, "ready": False}

    def grads(count):
        if not state["ready"]:
            state["ready"] = True
            for i in range(1, n_x):
                q = lax.rem(mq + i, n_x)
                remote(xall.at[q], xall.at[q], xs_sem.at[0], xr_sem.at[q], dp=lax.rem(mq + 1, n_x)).wait_recv()
                dd_desc(q).wait_recv()
        for s in range(state["slot"], min(state["slot"] + count, per_q)):
            lhs = jnp.concatenate([xall[q, s] for q in range(n_x)], axis=0)
            rhs = jnp.concatenate([ddall[q] for q in range(n_x)], axis=0)
            out = lax.dot_general(lhs, rhs, TN, preferred_element_type=F32)
            gg[0, feat * s : feat * (s + 1), :] = out[:, 0:ff].astype(BF16)
            gu[0, feat * s : feat * (s + 1), :] = out[:, ff : 2 * ff].astype(BF16)
        state["slot"] = min(state["slot"] + count, per_q)

    def give(j):
        contribute(1, 1, j)
        contribute(-1, 1, j)
        contribute(-1, 0, j)
        if j:
            contribute(1, 0, j - 1)

    def take(j):
        combine(1, 1, j)
        combine(-1, 1, j)
        combine(-1, 0, j)
        if j:
            combine(1, 0, j - 1)

    contribute(1, 0, K - 1)
    give(K - 1)
    for i in range(1, n_x):
        remote(ddall.at[mq], ddall.at[mq], dds_sem.at[0], ddr_sem.at[mq], dp=lax.rem(mq + i, n_x)).start()
    for j in range(K - 2, max(K - 4, -1), -1):
        give(j)
    combine(1, 0, K - 1)
    relay(1, K)
    take(K - 1)
    for j in range(K - 4, -1, -1):
        give(j)
    for j in range(K - 2, -1, -1):
        take(j)
        relay(1, j + 1)
        relay(-1, j + 1)
    grads(per_q)
    gt_ref[...] = relay_sum(1, 0) + relay_sum(-1, 0)

    for copy in sends:
        copy.wait_send()
    for sign in (1, -1):
        for part in (0, 1):
            for j in range(K):
                for dist in dists_of(sign, part, j):
                    if dist not in handed:
                        exchange_desc(dsp, rows, slot(sign, dist), ds_sem, dr_sem).wait_send()
                exchange_desc(cs, cr, span(sign, part, j), cs_sem, cr_sem).wait_send()
    if n_x > 1:
        part = pl.ds(0, n_x - 1)
        remote(xall.at[part], xall.at[part], xs_sem.at[0], xr_sem.at[0], dp=lax.rem(mq + 1, n_x)).wait_send()
        remote(ddall.at[part], ddall.at[part], dds_sem.at[0], ddr_sem.at[0], dp=lax.rem(mq + 1, n_x)).wait_send()


def body(tokens, grad_out, route_weights, expert_ids, w_gate, w_up, w_down):
    n_e, n_z, n_x = lax.axis_size("expert"), lax.axis_size("tensor"), lax.axis_size("dp")
    toks, feat = tokens.shape
    ff = w_gate.shape[2]
    width = w_gate.shape[1]
    cap = toks * expert_ids.shape[1] * 2 // n_e
    n_rows = n_e * cap
    S = STRIDE
    H = n_z // 2
    K = H // S
    per_q = n_z // n_x
    inputs = (tokens, grad_out, expert_ids.T, route_weights.T, w_gate, w_up, w_down)
    vmem = pl.BlockSpec(memory_space=pltpu.VMEM)
    hbm = pl.BlockSpec(memory_space=pl.ANY)
    dma = pltpu.SemaphoreType.DMA
    return pl.pallas_call(
        functools.partial(kernel, (n_e, n_z, n_x, cap)),
        name="moe_backward",
        out_shape=(
            jax.ShapeDtypeStruct((toks, feat), F32),
            jax.ShapeDtypeStruct((1, width // n_x, ff), BF16),
            jax.ShapeDtypeStruct((1, width // n_x, ff), BF16),
        ),
        in_specs=[hbm] * 7,
        out_specs=(vmem, vmem, vmem),
        scratch_shapes=[
            pltpu.VMEM(tokens.shape, BF16),
            pltpu.VMEM(tokens.shape, BF16),
            pltpu.VMEM(expert_ids.shape[::-1], jnp.int32),
            pltpu.VMEM(expert_ids.shape[::-1], F32),
            pltpu.VMEM((width, ff), BF16),
            pltpu.VMEM((width, ff), BF16),
            pltpu.VMEM((width, ff), BF16),
            pltpu.VMEM((H, toks, 2 * feat), BF16),
            pltpu.VMEM((H, toks, 2 * feat), BF16),
            pltpu.VMEM((2 * H, n_rows, 2 * feat), BF16),
            pltpu.VMEM((2 * H, n_rows, 2 * feat), BF16),
            pltpu.VMEM((n_rows, ff), F32),
            pltpu.VMEM((n_rows, ff), F32),
            pltpu.VMEM((n_rows, ff), F32),
            pltpu.VMEM((n_rows, 2 * ff), BF16),
            pltpu.VMEM((n_x, n_rows, 2 * ff), BF16),
            pltpu.VMEM((n_x, per_q, n_rows, feat), BF16),
            pltpu.VMEM((2 * H, n_rows, feat), BF16),
            pltpu.VMEM((2 * H, n_rows, feat), BF16),
            pltpu.VMEM((2, K, S, toks, feat), LINK),
            pltpu.VMEM((2, K, S, toks, feat), LINK),
            pltpu.VMEM((2, K, toks, feat), F32),
            dma((4,)), dma((3,)),
            dma((2, H)), dma((2, H)),
            dma((2 * H,)), dma((2 * H,)),
            dma((1,)), dma((n_x,)),
            dma((1,)), dma((n_x,)),
            dma((4 * K,)), dma((4 * K,)),
            dma((2, K, S)), dma((2, K, S)),
        ],
        compiler_params=pltpu.CompilerParams(collective_id=0, has_side_effects=True, vmem_limit_bytes=30 * 2**20),
    )(*[pltpu.with_memory_space_constraint(a, pltpu.HBM) for a in inputs])


def solution(mesh):
    placed = (
        P(("expert", "dp"), "tensor"),
        P(("expert", "dp"), "tensor"),
        P(("expert", "dp"), None),
        P(("expert", "dp"), None),
        P("expert", None, "tensor"),
        P("expert", None, "tensor"),
        P("expert", None, "tensor"),
    )
    return jax.shard_map(
        body,
        mesh=mesh,
        in_specs=placed,
        out_specs=(
            P(("expert", "dp"), "tensor"),
            P("expert", "dp", "tensor"),
            P("expert", "dp", "tensor"),
        ),
        check_vma=False,
    )
```

```python
import functools

import jax
import jax.numpy as jnp
from jax import lax
from jax.experimental import pallas as pl
from jax.experimental.pallas import tpu as pltpu
from jax.sharding import PartitionSpec as P

STRIDE = 4
LINK = jnp.bfloat16
F32 = jnp.float32
BF16 = jnp.bfloat16
NT = (((1,), (1,)), ((), ()))
TN = (((0,), (0,)), ((), ()))


def remote(src, dst, send_sem, recv_sem, **where):
    return pltpu.make_async_remote_copy(
        src_ref=src,
        dst_ref=dst,
        send_sem=send_sem,
        recv_sem=recv_sem,
        device_id=where,
        device_id_type=pl.DeviceIdType.MESH,
    )


def kernel(
    sizes,
    tok_hbm, dy_hbm, ids_hbm, rw_hbm, wg_hbm, wu_hbm, wd_hbm,
    gt_ref, gg_out, gu_out,
    tok_ref, dy_ref, ids_ref, rw_ref, wg, wu, wd, agp, agm, dsp, rows, acc_g, acc_u, acc_d, dd, ddall, xall,
    cs, cr, sbuf, rr, own, gg, gu,
    in_sem, w_sem, ag_ssem, ag_rsem, ds_sem, dr_sem, xs_sem, xr_sem, dds_sem, ddr_sem,
    cs_sem, cr_sem, rs_sem, rr_sem, out_sem,
):
    n_e, n_z, n_x, cap = sizes
    S = STRIDE
    H = n_z // 2
    K = H // S
    toks = tok_hbm.shape[0]
    feat = tok_hbm.shape[1]
    ff = wg.shape[1]
    n_rows = n_e * cap
    per_q = n_z // n_x
    me = lax.axis_index("expert")
    z = lax.axis_index("tensor")
    mq = lax.axis_index("dp")

    firsts = [
        pltpu.make_async_copy(src, dst, in_sem.at[i])
        for i, (src, dst) in enumerate(((tok_hbm, tok_ref), (dy_hbm, dy_ref), (ids_hbm, ids_ref), (rw_hbm, rw_ref)))
    ]
    for load in firsts:
        load.start()
    loads = [
        pltpu.make_async_copy(src.at[0], dst, w_sem.at[i])
        for i, (src, dst) in enumerate(((wg_hbm, wg), (wu_hbm, wu), (wd_hbm, wd)))
    ]
    for load in loads:
        load.start()

    barrier = pltpu.get_barrier_semaphore()
    partners = []
    for m in range(1, S + 1):
        partners.append({"tensor": lax.rem(z + m, n_z)})
        partners.append({"tensor": lax.rem(z + n_z - m, n_z)})
    for i in range(1, n_e):
        partners.append({"expert": lax.rem(me + i, n_e)})
    for i in range(1, n_x):
        partners.append({"dp": lax.rem(mq + i, n_x)})
    for where in partners:
        pl.semaphore_signal(barrier, inc=1, device_id=where, device_id_type=pl.DeviceIdType.MESH)

    for load in firsts[:2]:
        load.wait()
    agm[0, :, 0:feat] = tok_ref[...]
    agm[0, :, feat : 2 * feat] = dy_ref[...]

    pl.semaphore_wait(barrier, len(partners))

    def up(m):
        return lax.rem(z + m, n_z)

    def down(m):
        return lax.rem(z + n_z - m, n_z)

    def ag_copy(sign, j, m):
        dist = S * j + m
        if sign > 0:
            src = agm.at[0] if j == 0 else agp.at[S * j - 1]
            return remote(src, agp.at[dist - 1], ag_ssem.at[0], ag_rsem.at[0, dist - 1], tensor=up(m))
        return remote(agm.at[S * j], agm.at[dist], ag_ssem.at[0], ag_rsem.at[1, dist], tensor=down(m))

    def ag_wait(sign, dist):
        if sign > 0:
            remote(agp.at[dist - 1], agp.at[dist - 1], ag_ssem.at[0], ag_rsem.at[0, dist - 1], tensor=up(1)).wait_recv()
        elif dist > 0:
            remote(agm.at[dist], agm.at[dist], ag_ssem.at[0], ag_rsem.at[1, dist], tensor=up(1)).wait_recv()

    def span(sign, part, j):
        if part:
            first, count = S * j + 1, S - 1
        else:
            first, count = (S * (j + 1) if sign > 0 else S * j), 1
        at = first - 1 if sign > 0 else H + first
        return first, count, at, (0 if sign > 0 else 2 * K) + 2 * j + part

    def dists_of(sign, part, j):
        first, count, _, _ = span(sign, part, j)
        return list(range(first, first + count))

    me_rows = pl.ds(pl.multiple_of(me * cap, cap), cap)

    def exchange(src, dst, group, send_sem, recv_sem):
        _, count, at, g = group
        held = pl.ds(at, count)
        for i in range(1, n_e):
            e = lax.rem(me + i, n_e)
            copy = remote(
                src.at[held, pl.ds(pl.multiple_of(e * cap, cap), cap), :],
                dst.at[held, me_rows, :],
                send_sem.at[0], recv_sem.at[g], expert=e,
            )
            copy.start()
        dst[at : at + count, me_rows, :] = src[at : at + count, me_rows, :]

    def exchange_desc(src, dst, group, send_sem, recv_sem):
        _, count, at, g = group
        held, part = pl.ds(at, count), pl.ds(0, n_rows - cap)
        return remote(src.at[held, part, :], dst.at[held, part, :], send_sem.at[0], recv_sem.at[g],
                      expert=lax.rem(me + 1, n_e))

    handed = {S * j + S - 1 for j in range(K - 1)} if S > 2 else set()

    def hand_copy(sign, dist):
        at = slot(sign, dist)[2]
        return remote(rows.at[slot(sign, dist - 1)[2]], rows.at[at], ds_sem.at[1], dr_sem.at[at],
                      tensor=(up if sign > 0 else down)(1))

    arrived = set()

    def await_rows(sign, dist):
        if (sign, dist) in arrived:
            return
        arrived.add((sign, dist))
        if dist in handed:
            hand_copy(sign, dist).wait_recv()
        else:
            exchange_desc(dsp, rows, slot(sign, dist), ds_sem, dr_sem).wait_recv()

    def hand(sign, dist):
        await_rows(sign, dist - 1)
        copy = hand_copy(sign, dist)
        copy.start()

    def slot(sign, dist):
        at = dist - 1 if sign > 0 else H + dist
        return dist, 1, at, at

    def dispatch(sign, dist):
        group = slot(sign, dist)
        at = group[2]
        picked = jnp.dot(pick, agp[dist - 1] if sign > 0 else agm[dist], preferred_element_type=F32)
        dsp[at, :, 0:feat] = picked[:, 0:feat].astype(BF16)
        dsp[at, :, feat : 2 * feat] = (picked[:, feat : 2 * feat] * p_col).astype(BF16)
        exchange(dsp, rows, group, ds_sem, dr_sem)

    started = []

    def consume(sign, j):
        parts = (1, 0) if sign > 0 else (0, 1)
        dists = [dist for part in parts for dist in dists_of(sign, part, j)]
        for dist in dists:
            await_rows(sign, dist)
        at0 = slot(sign, dists[0])[2]
        if not started:
            for load in loads:
                load.wait()
        places = [down(dist) if sign > 0 else up(dist) for dist in dists]
        x = jnp.concatenate([rows[at0 + s, :, 0:feat] for s in range(S)], axis=1)
        d = jnp.concatenate([rows[at0 + s, :, feat : 2 * feat] for s in range(S)], axis=1)

        def slab(w):
            return jnp.concatenate(
                [w[pl.ds(pl.multiple_of(at * feat, feat), feat), :] for at in places], axis=0)

        for lhs, w, acc in ((x, wg, acc_g), (x, wu, acc_u), (d, wd, acc_d)):
            term = jnp.dot(lhs, slab(w), preferred_element_type=F32)
            acc[...] = term if not started else acc[...] + term
        started.append(True)
        for s, at in enumerate(places):
            to = at // per_q
            local = lax.rem(at, per_q)

            @pl.when(to == mq)
            def _():
                xall[mq, local] = rows[at0 + s, :, 0:feat]

            if n_x > 1:
                @pl.when(to != mq)
                def _():
                    remote(rows.at[at0 + s, :, pl.ds(0, feat)], xall.at[mq, local], xs_sem.at[0],
                           xr_sem.at[mq], dp=to).start()

    def ag_send(sign, j, m):
        if sign > 0 or S * j + m < H:
            copy = ag_copy(sign, j, m)
            copy.start()

    def ag_step(j):
        for sign in (1, -1):
            if j:
                ag_wait(sign, S * j)
            ag_send(sign, j, S)
        for m in range(1, S):
            for sign in (1, -1):
                if S * j + m not in handed:
                    ag_send(sign, j, m)

    def spread(j):
        if j:
            dispatch(1, S * j)
        dispatch(-1, S * j)
        for m in range(1, S):
            for sign in (1, -1):
                if S * j + m not in handed:
                    ag_wait(sign, S * j + m)
                    dispatch(sign, S * j + m)
        if j and S * j - 1 in handed:
            for sign in (1, -1):
                hand(sign, S * j - 1)

    ag_step(0)
    for load in firsts[2:]:
        load.wait()
    row = lax.broadcasted_iota(jnp.int32, (n_rows, toks), 0)
    row_expert = row // cap
    row_slot = (row - row_expert * cap).astype(F32)
    first = ids_ref[0:1, :] == row_expert
    second = ids_ref[1:2, :] == row_expert
    named = jnp.where(first, 1.0, jnp.where(second, 1.0, 0.0)).astype(F32)
    before = lax.broadcasted_iota(jnp.int32, (toks, toks), 0)
    after = lax.broadcasted_iota(jnp.int32, (toks, toks), 1)
    earlier = jnp.where(before < after, 1.0, 0.0).astype(BF16)
    place = jnp.dot(named.astype(BF16), earlier, preferred_element_type=F32)
    pick_f = jnp.where(place == row_slot, named, 0.0)
    weight = jnp.where(first, rw_ref[0:1, :], rw_ref[1:2, :])
    p_col = jnp.sum(pick_f * weight, axis=1, keepdims=True)
    pick = pick_f.astype(BF16)
    eye = jnp.where(before == after, 1.0, 0.0).astype(BF16)
    pick_back = lax.dot_general(eye, pick, NT, preferred_element_type=F32).astype(BF16)

    spread(0)
    for j in range(1, K):
        ag_step(j)
        spread(j)
    for j in range(K // 2):
        consume(-1, j)
        consume(1, j)
    ag_wait(1, H)
    dispatch(1, H)
    for j in range(K // 2, K):
        consume(-1, j)
        consume(1, j)

    gate_pre = acc_g[...]
    up_pre = acc_u[...]
    d_hidden = acc_d[...]
    sig = jax.nn.sigmoid(gate_pre)
    d_up = (d_hidden * (gate_pre * sig)).astype(BF16)
    d_gate = (d_hidden * up_pre * sig * (1.0 + gate_pre * (1.0 - sig))).astype(BF16)
    dd[:, 0:ff] = d_gate
    dd[:, ff : 2 * ff] = d_up
    ddall[mq] = dd[...]

    def contribute(sign, part, j):
        group = span(sign, part, j)
        _, count, at, _ = group
        places = [up(dist) if sign > 0 else down(dist) for dist in dists_of(sign, part, j)]

        def slab(w):
            slabs = [w[pl.ds(pl.multiple_of(to * feat, feat), feat), :] for to in places]
            return jnp.concatenate(slabs, axis=0) if count > 1 else slabs[0]

        term = lax.dot_general(dd[:, 0:ff], slab(wg), NT, preferred_element_type=F32)
        term = term + lax.dot_general(dd[:, ff : 2 * ff], slab(wu), NT, preferred_element_type=F32)
        for s in range(count):
            cs[at + s] = term[:, feat * s : feat * (s + 1)].astype(BF16)
        exchange(cs, cr, group, cs_sem, cr_sem)

    def ring_copy(sign, j, m):
        where = (up if sign > 0 else down)(S if m == 0 else m)
        d = 0 if sign > 0 else 1
        return remote(sbuf.at[d, j, m], rr.at[d, j, m], rs_sem.at[0], rr_sem.at[d, j, m], tensor=where)

    def combine(sign, part, j):
        group = span(sign, part, j)
        _, count, at, _ = group
        d = 0 if sign > 0 else 1
        exchange_desc(cs, cr, group, cs_sem, cr_sem).wait_recv()
        wide = jnp.concatenate([cr[at + s] for s in range(count)], axis=1) if count > 1 else cr[at]
        comb = jnp.dot(pick_back, wide, preferred_element_type=F32)
        if not part:
            own[d, j] = comb
            return
        for s in range(count):
            sbuf[d, j, s + 1] = comb[:, feat * s : feat * (s + 1)].astype(LINK)
            copy = ring_copy(sign, j, s + 1)
            copy.start()

    def relay_sum(sign, j):
        d = 0 if sign > 0 else 1
        total = None
        if sign > 0 and j > 0:
            total = own[0, j - 1]
        elif sign < 0:
            total = own[1, j]
        if j < K:
            for l in range(1, S):
                ring_copy(sign, j, l).wait_recv()
                piece = rr[d, j, l].astype(F32)
                total = piece if total is None else total + piece
            if sign > 0 or j < K - 1:
                ring_copy(sign, j, 0).wait_recv()
                piece = rr[d, j, 0].astype(F32)
                total = piece if total is None else total + piece
        return total

    def relay(sign, j):
        d = 0 if sign > 0 else 1
        total = relay_sum(sign, j)
        sbuf[d, j - 1, 0] = total.astype(LINK)
        copy = ring_copy(sign, j - 1, 0)
        copy.start()

    def dd_desc(q):
        return remote(ddall.at[q], ddall.at[q], dds_sem.at[0], ddr_sem.at[q], dp=lax.rem(mq + 1, n_x))

    state = {"slot": 0, "ready": False}

    def grads(count):
        if not state["ready"]:
            state["ready"] = True
            for i in range(1, n_x):
                q = lax.rem(mq + i, n_x)
                remote(xall.at[q], xall.at[q], xs_sem.at[0], xr_sem.at[q], dp=lax.rem(mq + 1, n_x)).wait_recv()
                dd_desc(q).wait_recv()
        for s in range(state["slot"], min(state["slot"] + count, per_q)):
            lhs = jnp.concatenate([xall[q, s] for q in range(n_x)], axis=0)
            rhs = jnp.concatenate([ddall[q] for q in range(n_x)], axis=0)
            out = lax.dot_general(lhs, rhs, TN, preferred_element_type=F32)
            gg[0, feat * s : feat * (s + 1), :] = out[:, 0:ff].astype(BF16)
            gu[0, feat * s : feat * (s + 1), :] = out[:, ff : 2 * ff].astype(BF16)
        state["slot"] = min(state["slot"] + count, per_q)

    def give(j):
        contribute(1, 1, j)
        contribute(-1, 1, j)
        contribute(-1, 0, j)
        if j:
            contribute(1, 0, j - 1)

    def take(j):
        combine(1, 1, j)
        combine(-1, 1, j)
        combine(-1, 0, j)
        if j:
            combine(1, 0, j - 1)

    contribute(1, 0, K - 1)
    give(K - 1)
    for i in range(1, n_x):
        remote(ddall.at[mq], ddall.at[mq], dds_sem.at[0], ddr_sem.at[mq], dp=lax.rem(mq + i, n_x)).start()
    for j in range(K - 2, max(K - 4, -1), -1):
        give(j)
    combine(1, 0, K - 1)
    relay(1, K)
    take(K - 1)
    for j in range(K - 4, -1, -1):
        give(j)
    for j in range(K - 2, -1, -1):
        take(j)
        relay(1, j + 1)
        relay(-1, j + 1)
    grads(per_q)
    outs = [
        pltpu.make_async_copy(gg, gg_out, out_sem.at[0]),
        pltpu.make_async_copy(gu, gu_out, out_sem.at[1]),
    ]
    for copy in outs:
        copy.start()
    gt_ref[...] = relay_sum(1, 0) + relay_sum(-1, 0)

    n_hand = 2 * len(handed)

    def drain(ref, sem, other):
        remote(ref, ref, sem, other, tensor=up(1)).wait_send()

    drain(dsp.at[pl.ds(0, 2 * H - 1 - n_hand), pl.ds(0, toks), :], ag_ssem.at[0], ag_rsem.at[0, 0])
    drain(dsp.at[pl.ds(0, 2 * H - n_hand), pl.ds(0, n_rows - cap), :], ds_sem.at[0], dr_sem.at[0])
    if n_hand:
        drain(dsp.at[pl.ds(0, n_hand), :, :], ds_sem.at[1], dr_sem.at[0])
    drain(cs.at[pl.ds(0, 2 * H), pl.ds(0, n_rows - cap), :], cs_sem.at[0], cr_sem.at[0])
    drain(cs.at[pl.ds(0, 2 * H - 1), pl.ds(0, toks), :], rs_sem.at[0], rr_sem.at[0, 0, 0])
    if n_x > 1:
        part = pl.ds(0, n_x - 1)
        remote(xall.at[part], xall.at[part], xs_sem.at[0], xr_sem.at[0], dp=lax.rem(mq + 1, n_x)).wait_send()
        remote(ddall.at[part], ddall.at[part], dds_sem.at[0], ddr_sem.at[0], dp=lax.rem(mq + 1, n_x)).wait_send()
    for copy in outs:
        copy.wait()


def body(tokens, grad_out, route_weights, expert_ids, w_gate, w_up, w_down):
    n_e, n_z, n_x = lax.axis_size("expert"), lax.axis_size("tensor"), lax.axis_size("dp")
    toks, feat = tokens.shape
    ff = w_gate.shape[2]
    width = w_gate.shape[1]
    cap = toks * expert_ids.shape[1] * 2 // n_e
    n_rows = n_e * cap
    S = STRIDE
    H = n_z // 2
    K = H // S
    per_q = n_z // n_x
    inputs = (tokens, grad_out, expert_ids.T, route_weights.T, w_gate, w_up, w_down)
    vmem = pl.BlockSpec(memory_space=pltpu.VMEM)
    anywhere = pl.BlockSpec(memory_space=pl.ANY)
    hbm = pl.BlockSpec(memory_space=pl.ANY)
    dma = pltpu.SemaphoreType.DMA
    return pl.pallas_call(
        functools.partial(kernel, (n_e, n_z, n_x, cap)),
        name="moe_backward",
        out_shape=(
            jax.ShapeDtypeStruct((toks, feat), F32),
            jax.ShapeDtypeStruct((1, width // n_x, ff), BF16),
            jax.ShapeDtypeStruct((1, width // n_x, ff), BF16),
        ),
        in_specs=[hbm] * 7,
        out_specs=(vmem, anywhere, anywhere),
        scratch_shapes=[
            pltpu.VMEM(tokens.shape, BF16),
            pltpu.VMEM(tokens.shape, BF16),
            pltpu.VMEM(expert_ids.shape[::-1], jnp.int32),
            pltpu.VMEM(expert_ids.shape[::-1], F32),
            pltpu.VMEM((width, ff), BF16),
            pltpu.VMEM((width, ff), BF16),
            pltpu.VMEM((width, ff), BF16),
            pltpu.VMEM((H, toks, 2 * feat), BF16),
            pltpu.VMEM((H, toks, 2 * feat), BF16),
            pltpu.VMEM((2 * H, n_rows, 2 * feat), BF16),
            pltpu.VMEM((2 * H, n_rows, 2 * feat), BF16),
            pltpu.VMEM((n_rows, ff), F32),
            pltpu.VMEM((n_rows, ff), F32),
            pltpu.VMEM((n_rows, ff), F32),
            pltpu.VMEM((n_rows, 2 * ff), BF16),
            pltpu.VMEM((n_x, n_rows, 2 * ff), BF16),
            pltpu.VMEM((n_x, per_q, n_rows, feat), BF16),
            pltpu.VMEM((2 * H, n_rows, feat), BF16),
            pltpu.VMEM((2 * H, n_rows, feat), BF16),
            pltpu.VMEM((2, K, S, toks, feat), LINK),
            pltpu.VMEM((2, K, S, toks, feat), LINK),
            pltpu.VMEM((2, K, toks, feat), F32),
            pltpu.VMEM((1, width // n_x, ff), BF16),
            pltpu.VMEM((1, width // n_x, ff), BF16),
            dma((4,)), dma((3,)),
            dma((1,)), dma((2, H)),
            dma((2,)), dma((2 * H,)),
            dma((1,)), dma((n_x,)),
            dma((1,)), dma((n_x,)),
            dma((1,)), dma((4 * K,)),
            dma((1,)), dma((2, K, S)),
            dma((2,)),
        ],
        compiler_params=pltpu.CompilerParams(collective_id=0, has_side_effects=True, vmem_limit_bytes=30 * 2**20),
    )(*[pltpu.with_memory_space_constraint(a, pltpu.HBM) for a in inputs])


def solution(mesh):
    placed = (
        P(("expert", "dp"), "tensor"),
        P(("expert", "dp"), "tensor"),
        P(("expert", "dp"), None),
        P(("expert", "dp"), None),
        P("expert", None, "tensor"),
        P("expert", None, "tensor"),
        P("expert", None, "tensor"),
    )
    return jax.shard_map(
        body,
        mesh=mesh,
        in_specs=placed,
        out_specs=(
            P(("expert", "dp"), "tensor"),
            P("expert", "dp", "tensor"),
            P("expert", "dp", "tensor"),
        ),
        check_vma=False,
    )
```
